512 devices in a mesh: slab: 64 (over z_lo, x, core), grp: 8 (over z_hi, y).
Axes of the slice: x: 4, y: 4, z: 16 (z_hi: 2, z_lo: 8; z = z_hi * 8 + z_lo), core: 2. Of those that a mesh axis runs over, the one named last changes fastest.
Arguments:
- adj_out: float32 [5, 512, 256, 256], P(None, 'grp', 'slab'), may hold values from -6 to 6
- advect: bfloat16 [3, 512, 256, 256], P(None, 'grp', 'slab'), may hold values from -4 to 4
- viscosity: bfloat16 [512, 256, 256], P('grp', 'slab'), may hold values from 0.099609375 to 0.796875
- body_mask: int32 [512, 256, 256], P('grp', 'slab'), may hold values 0 or 1
- marker_x: int32 [2048], replicated, may hold values from 128 to 191
- marker_z: int32 [2048], replicated, may hold values from 0 to 255
- marker_y: int32 [2048], replicated, may hold values from 64 to 191
- drag_weight: float32 [2048], replicated, may hold values from -5 to 5
- inv_x: float32 [512, 512], P(None, 'grp'), may hold values from 0 to 1, as said below
- inv_y: float32 [256, 256], replicated, may hold values from 0 to 1, as said below
- inv_z: float32 [256, 256], replicated, may hold values from 0 to 1, as said below
Outputs:
- state_adjoint: float32 [5, 512, 256, 256], P(None, 'grp', 'slab')
The draws below stay inside these ranges and needn't reach their ends.
Inputs may be any that keep to these rules, and one draw needn't show every extreme that they name: `inv_x`: entries of a given inverse. `inv_y`: entries of a given inverse. `inv_z`: entries of a given inverse.
All inputs are finite; a program needn't handle non-finite values. No bound on the sum of `body_mask` on one device may be relied on, other than what follows from the above.
Results may differ from the reference program's by a relative error of at most 0.0003.
Values sent between devices are 32-bit elements; how exact they have to be, the bound alone decides.
No kernel may reach another device: no remote copies, remote signals or barrier semaphores. Data moves between devices by JAX's collectives and lax.ppermute only.
A program may use at most 64 MiB of HBM per device.

```python
import math
from functools import partial
import jax
import jax.numpy as jnp
from jax import lax

FIELDS = 5
NY = 256
MARKERS = 2048
NX = 512
NZ = 256


def line_inverse(key, count):
    reach = count / 4.0
    rows_idx = jnp.arange(count)[:, None]
    cols_idx = jnp.arange(count)[None, :]
    apart = jnp.abs(rows_idx - cols_idx).astype(jnp.float32)
    noise = jnp.clip(jax.random.normal(key, (count, count), jnp.float32), -2.0, 2.0) * 0.5
    spread = 0.2 / reach * jnp.exp(-apart / reach) * (1.0 + 0.5 * noise)
    return 0.6 * jnp.eye(count, dtype=jnp.float32) + spread


def draw_inv_x(key, part):
    return line_inverse(jax.random.fold_in(key, 11), NX)


def draw_inv_y(key, part):
    return line_inverse(jax.random.fold_in(key, 23), NY)


def draw_inv_z(key, part):
    return line_inverse(jax.random.fold_in(key, 37), NZ)


def with_ends(values, stream_key, least, largest):
    spot = [jax.random.randint(jax.random.fold_in(stream_key, axis), (), 0, length) for axis, length in enumerate(values.shape)]
    widest = values.shape.index(max(values.shape))
    beside = spot[:widest] + [(spot[widest] + 1) % values.shape[widest]] + spot[widest + 1:]
    return values.at[tuple(spot)].set(least).at[tuple(beside)].set(largest)


def block_levels(stream_key, extent, shards, least, top_value):
    loudness = 1.0
    for axis_at, shards_of in shards:
        draws = jax.random.uniform(jax.random.fold_in(jax.random.fold_in(stream_key, 6), axis_at), (shards_of,), jnp.float32, least / len(shards), top_value / len(shards))
        loudness = loudness * jnp.repeat(jnp.exp(draws), extent[axis_at] // shards_of).reshape((-1,) + (1,) * (len(extent) - 1 - axis_at))
    return loudness


def normal_values(key, dims, scale, limit, pieces=(), kind=jnp.bfloat16):
    values = scale * jax.random.normal(key, dims, jnp.float32)
    if pieces:
        values = values * block_levels(key, dims, pieces, -0.22, 0.18)
    return jnp.clip(values, -limit, limit).astype(kind)


def setup_inputs(seed: int = 0) -> dict:
    splits = jax.random.split(jax.random.key(seed), 12)
    return {
        "adj_out": normal_values(splits[0], (FIELDS, NX, NZ, NY), 1.0, 6.0, ((1, 8), (2, 64)), jnp.float32),
        "advect": normal_values(splits[1], (3, NX, NZ, NY), 1.0, 4.0, ((1, 8), (2, 64))),
        "viscosity": jnp.clip(jnp.exp(math.log(0.796875) - 2.0794415 * jax.random.uniform(splits[2], (NX, NZ, NY), jnp.float32) ** block_levels(splits[2], (NX, NZ, NY), ((0, 8), (1, 64)), -0.2, 0.2)), 0.099609375, 0.796875).astype(jnp.bfloat16),
        "body_mask": with_ends((jax.random.randint(splits[3], (NX, NZ, NY), 0, 10) < 9).astype(jnp.int32), jax.random.fold_in(splits[3], 1), 0, 1),
        "marker_x": with_ends(jax.random.randint(splits[4], (MARKERS,), NX // 4, NX // 4 + NX // 8), jax.random.fold_in(splits[4], 1), NX // 4, (NX // 4 + NX // 8) - 1).astype(jnp.int32),
        "marker_z": with_ends(jax.random.randint(splits[5], (MARKERS,), 0, NZ), jax.random.fold_in(splits[5], 1), 0, NZ - 1).astype(jnp.int32),
        "marker_y": with_ends(jax.random.randint(splits[6], (MARKERS,), NY // 4, 3 * NY // 4), jax.random.fold_in(splits[6], 1), NY // 4, (3 * NY // 4) - 1).astype(jnp.int32),
        "drag_weight": normal_values(splits[7], (MARKERS,), 1.0, 5.0, (), jnp.float32),
        "inv_x": draw_inv_x(jax.random.fold_in(splits[11], 71), 0),
        "inv_y": draw_inv_y(jax.random.fold_in(splits[11], 71), 0),
        "inv_z": draw_inv_z(jax.random.fold_in(splits[11], 71), 0),
    }


time_step = 0.08
highest = lax.Precision.HIGHEST


def adjoint_field(inv_x, inv_y, inv_z, masking, velocity, viscous, field):
    solved = jnp.einsum("jk,xjy->xky", inv_z, field, precision=highest)
    solved = jnp.einsum("jk,xzj->xzk", inv_y, solved, precision=highest)
    solved = jnp.einsum("jk,jzy->kzy", inv_x, solved, precision=highest)
    masked = solved * masking
    padded = jnp.pad(masked, 1)
    centre = padded[1:-1, 1:-1, 1:-1]
    grad_x = (padded[2:, 1:-1, 1:-1] - padded[:-2, 1:-1, 1:-1]) * 0.5
    grad_z = (padded[1:-1, 2:, 1:-1] - padded[1:-1, :-2, 1:-1]) * 0.5
    grad_y = (padded[1:-1, 1:-1, 2:] - padded[1:-1, 1:-1, :-2]) * 0.5
    laplace = (padded[2:, 1:-1, 1:-1] + padded[:-2, 1:-1, 1:-1]
               + padded[1:-1, 2:, 1:-1] + padded[1:-1, :-2, 1:-1]
               + padded[1:-1, 1:-1, 2:] + padded[1:-1, 1:-1, :-2] - 6.0 * centre)
    change = velocity[0] * grad_x + velocity[1] * grad_z + velocity[2] * grad_y + viscous * laplace
    return centre + time_step * change


def reference(adj_out, advect, viscosity, body_mask, marker_x, marker_z, marker_y, drag_weight, inv_x, inv_y, inv_z):
    seeded = adj_out.at[0, marker_x, marker_z, marker_y].add(drag_weight.astype(adj_out.dtype))
    masking = body_mask.astype(adj_out.dtype)
    velocity = advect.astype(adj_out.dtype)
    viscous = viscosity.astype(adj_out.dtype)
    worker = partial(adjoint_field, inv_x, inv_y, inv_z, masking, velocity, viscous)
    return lax.map(worker, seeded)
```

```python
import jax
import jax.numpy as jnp
from jax import lax
from jax.sharding import Mesh, PartitionSpec as P

time_step = 0.08
highest = lax.Precision.HIGHEST
chips = ("zl", "xx", "zh", "yy")
slab = ("zl", "xx", "co")
grp = ("zh", "yy")


def whole_inv_x(inv_x):
    rows, cols = inv_x.shape
    x_size, c_size = lax.axis_size("xx"), lax.axis_size("co")
    pieces = x_size * c_size
    depth = rows // pieces
    piece = lax.axis_index(("xx", "co"))
    mine = lax.dynamic_slice_in_dim(inv_x, piece * depth, depth, axis=0)
    theirs = lax.ppermute(mine, "zh", [(0, 1), (1, 0)])
    low = lax.axis_index("zh") == 0
    pair = jnp.stack([jnp.where(low, mine, theirs), jnp.where(low, theirs, mine)])
    gathered = lax.all_gather(pair, ("xx", "co", "yy"), axis=0, tiled=False)
    gathered = gathered.reshape(pieces, lax.axis_size("yy"), 2, depth, cols)
    return gathered.transpose(0, 3, 2, 1, 4).reshape(rows, rows)


def pushes(marker_x, marker_z, marker_y, drag_weight, x_rows, z_rows, y_cells):
    x_offset = lax.axis_index(grp) * x_rows
    z_offset = lax.axis_index(slab) * z_rows
    local_x = marker_x - x_offset
    local_z = marker_z - z_offset
    inside = (local_x >= 0) & (local_x < x_rows) & (local_z >= 0) & (local_z < z_rows)
    cell = jnp.where(inside, local_x * z_rows + local_z, -1)
    cells = lax.broadcasted_iota(jnp.int32, (x_rows * z_rows, 1), 0)
    here = (cells == cell[None, :]).astype(jnp.float32)
    lanes = lax.broadcasted_iota(jnp.int32, (1, y_cells), 1)
    weighted = jnp.where(marker_y[:, None] == lanes, drag_weight[:, None], 0.0)
    out = jnp.dot(here, weighted, precision=highest)
    return out.reshape(x_rows, z_rows, y_cells)


def neighbours(cells, axes, dim):
    count = lax.axis_size(axes)
    head = lax.slice_in_dim(cells, 0, 1, axis=dim)
    tail = lax.slice_in_dim(cells, cells.shape[dim] - 1, cells.shape[dim], axis=dim)
    before = lax.ppermute(tail, axes, [(i, i + 1) for i in range(count - 1)])
    after = lax.ppermute(head, axes, [(i + 1, i) for i in range(count - 1)])
    return before, after


def body(
    adj_out,
    advect,
    viscosity,
    body_mask,
    marker_x,
    marker_z,
    marker_y,
    drag_weight,
    inv_x,
    inv_y,
    inv_z,
):
    fields, x_rows, z_rows, y_cells = adj_out.shape
    zl, xx, co, zh, yy = (lax.axis_size(a) for a in ("zl", "xx", "co", "zh", "yy"))
    full_x = whole_inv_x(inv_x)
    pushed = pushes(marker_x, marker_z, marker_y, drag_weight, x_rows, z_rows, y_cells)
    seeded = adj_out.at[0].add(pushed)
    ysolved = jnp.einsum("lm,cxzl->mcxz", inv_y, seeded, precision=highest)
    sent = ysolved.reshape(y_cells, fields * x_rows * z_rows)
    got = lax.all_to_all(sent, chips, split_axis=0, concat_axis=0, tiled=True)
    got = got.reshape(zl * xx, zh * yy, fields, x_rows, z_rows)
    mine = got.transpose(2, 1, 3, 0, 4).reshape(fields, zh * yy * x_rows, zl * xx * z_rows)
    theirs = lax.ppermute(mine, "co", [(0, 1), (1, 0)])
    core = lax.axis_index("co")
    by_core = inv_z.reshape(zl * xx, co, z_rows, zl * xx, co, z_rows)
    to_me = lax.dynamic_index_in_dim(by_core, core, axis=4, keepdims=False)
    half = zl * xx * z_rows
    own = lax.dynamic_index_in_dim(to_me, core, axis=1, keepdims=False).reshape(half, half)
    other = lax.dynamic_index_in_dim(to_me, 1 - core, axis=1, keepdims=False).reshape(half, half)
    zsolved = jnp.einsum("cxj,jk->cxk", mine, own, precision=highest) + jnp.einsum(
        "cxj,jk->cxk", theirs, other, precision=highest
    )
    xsolved = jnp.einsum("cjz,jk->ckz", zsolved, full_x, precision=highest)
    back = xsolved.reshape(fields, zh * yy, x_rows, zl * xx, z_rows).transpose(3, 1, 0, 2, 4)
    back = back.reshape(y_cells, fields * x_rows * z_rows)
    solved = lax.all_to_all(back, chips, split_axis=0, concat_axis=0, tiled=True)
    solved = solved.T.reshape(fields, x_rows, z_rows, y_cells)
    masked = solved * body_mask.astype(jnp.float32)
    x_before, x_after = neighbours(masked, grp, 1)
    z_before, z_after = neighbours(masked, slab, 2)
    x_less = jnp.concatenate([x_before, masked[:, :-1]], axis=1)
    x_more = jnp.concatenate([masked[:, 1:], x_after], axis=1)
    z_less = jnp.concatenate([z_before, masked[:, :, :-1]], axis=2)
    z_more = jnp.concatenate([masked[:, :, 1:], z_after], axis=2)
    y_padded = jnp.pad(masked, ((0, 0), (0, 0), (0, 0), (1, 1)))
    y_less, y_more = y_padded[..., :-2], y_padded[..., 2:]
    grad_x = (x_more - x_less) * 0.5
    grad_z = (z_more - z_less) * 0.5
    grad_y = (y_more - y_less) * 0.5
    laplace = x_more + x_less + z_more + z_less + y_more + y_less - 6.0 * masked
    velocity = advect.astype(jnp.float32)
    viscous = viscosity.astype(jnp.float32)
    change = velocity[0] * grad_x + velocity[1] * grad_z + velocity[2] * grad_y + viscous * laplace
    return masked + time_step * change


def solution(mesh):
    fine = Mesh(mesh.devices.reshape(8, 4, 2, 2, 4), ("zl", "xx", "co", "zh", "yy"))
    field = P(None, grp, slab, None)
    in_specs = (field, field, P(grp, slab, None), P(grp, slab, None), P(), P(), P(), P(), P(None, grp), P(), P())
    return jax.shard_map(body, mesh=fine, in_specs=in_specs, out_specs=field, check_vma=False)
```

```python
import functools

import jax
import jax.numpy as jnp
from jax import lax
from jax.experimental import pallas as pl
from jax.experimental.pallas import tpu as pltpu
from jax.sharding import Mesh, PartitionSpec as P


time_step = 0.08
highest = lax.Precision.HIGHEST
chips = ("zl", "xx", "zh", "yy")
slab = ("zl", "xx", "co")
grp = ("zh", "yy")
swap = [(0, 1), (1, 0)]


def parts(value):
    high = value.astype(jnp.bfloat16)
    return high, (value - high.astype(jnp.float32)).astype(jnp.bfloat16)


def product(left, right):
    dot = functools.partial(jnp.dot, preferred_element_type=jnp.float32)
    return dot(left[0], right[0]) + (dot(left[0], right[1]) + dot(left[1], right[0]))


def gather_ring(block, axis):
    count = lax.axis_size(axis)
    me = lax.axis_index(axis)
    out = jnp.zeros((count,) + block.shape, block.dtype)
    out = lax.dynamic_update_index_in_dim(out, block, me, 0)
    for hop in range(1, count):
        from_it = lax.ppermute(block, axis, [(i, (i + hop) % count) for i in range(count)])
        out = lax.dynamic_update_index_in_dim(out, from_it, (me - hop) % count, 0)
    return out


def inv_x_pair(inv_x):
    pieces = lax.axis_size("xx") * lax.axis_size("co")
    depth = inv_x.shape[0] // pieces
    mine = lax.dynamic_slice_in_dim(inv_x, lax.axis_index(("xx", "co")) * depth, depth, axis=0)
    theirs = lax.ppermute(mine, "zh", swap)
    low = lax.axis_index("zh") == 0
    return jnp.concatenate([jnp.where(low, mine, theirs), jnp.where(low, theirs, mine)], axis=1)


def whole_inv_x(pair):
    for axis in ("co", "xx", "yy"):
        pair = gather_ring(pair, axis)
    return pair.reshape(pair.shape[0], -1, pair.shape[-1])


def pushes(marker_x, marker_z, marker_y, drag_weight, x_rows, z_rows, y_cells):
    x_offset = lax.axis_index(grp) * x_rows
    z_offset = lax.axis_index(slab) * z_rows
    local_x = marker_x - x_offset
    local_z = marker_z - z_offset
    inside = (local_x >= 0) & (local_x < x_rows) & (local_z >= 0) & (local_z < z_rows)
    cell = jnp.where(inside, local_x * z_rows + local_z, -1)
    cells = lax.broadcasted_iota(jnp.int32, (x_rows * z_rows, 1), 0)
    here = (cells == cell[None, :]).astype(jnp.float32)
    lanes = lax.broadcasted_iota(jnp.int32, (1, y_cells), 1)
    weighted = jnp.where(marker_y[:, None] == lanes, drag_weight[:, None], 0.0)
    out = jnp.dot(here, weighted, precision=highest)
    return out.reshape(x_rows, z_rows, y_cells)


def z_weights(inv_z, z_rows):
    count = inv_z.shape[0]
    half = count // 2
    groups = half // z_rows
    core = lax.axis_index("co")

    def chosen(which):
        k = lax.broadcasted_iota(jnp.int32, (half, count), 0)
        z = lax.broadcasted_iota(jnp.int32, (half, count), 1)
        return (z == (k % groups) * (2 * z_rows) + which * z_rows + k // groups).astype(jnp.float32)

    mine = chosen(core)
    both = jnp.concatenate([mine, chosen(1 - core)], axis=0)
    picked = jnp.einsum("az,zw->aw", both, inv_z, precision=highest)
    return jnp.einsum("bw,aw->ba", mine, picked, precision=highest)


def solve_kernel(fields, own_ref, other_ref, wz_high, wz_low, ix_high, ix_low, out_ref, z_ref, edge_ref):
    rows = own_ref.shape[0] // 256
    out_rows = out_ref.shape[0] // 256
    lane = lax.broadcasted_iota(jnp.int32, (32, 128), 1)
    low_half = lane < 64

    def lines(ref, c):
        evens, odds = [None, None], [None, None]
        for pair in range(2):
            even, odd = [], []
            for q in range(4):
                at = q * rows + 2 * c + pair
                first = ref[pl.ds(at, 32, stride=8 * rows), :]
                second = ref[pl.ds(at + 4 * rows, 32, stride=8 * rows), :]
                even.append(jnp.where(low_half, first, pltpu.roll(second, 64, 1)))
                odd.append(jnp.where(low_half, pltpu.roll(first, 64, 1), second))
            evens[pair] = jnp.concatenate(even, axis=1)
            odds[pair] = jnp.concatenate(odd, axis=1)
        return jnp.concatenate([evens[0], odds[0], evens[1], odds[1]], axis=0)

    wz = wz_high[...], wz_low[...]
    for c in range(fields):
        both = jnp.concatenate([lines(own_ref, c), lines(other_ref, c)], axis=0)
        z_ref[pl.ds(c * 128, 128), :] = product(wz, parts(both))
    ix = ix_high[...], ix_low[...]
    edge_ref[...] = jnp.zeros_like(edge_ref)
    for c in range(fields):
        done = product(parts(z_ref[pl.ds(c * 128, 128), :]), ix)
        for pair in range(2):
            for q in range(4):
                two = [done[(2 * pair + i) * 32 : (2 * pair + i + 1) * 32, q * 128 : q * 128 + 128] for i in range(2)]
                at = q * out_rows + 2 * c + pair
                first = jnp.where(low_half, two[0], pltpu.roll(two[1], 64, 1))
                second = jnp.where(low_half, pltpu.roll(two[0], 64, 1), two[1])
                out_ref[pl.ds(at, 32, stride=8 * out_rows), :] = first
                out_ref[pl.ds(at + 4 * out_rows, 32, stride=8 * out_rows), :] = second
                for i in range(2):
                    k = c * 4 + 2 * pair + i
                    outer = pltpu.roll(two[i], 2 * k + 1, 1)
                    inner = pltpu.roll(two[i], (2 * k + 65) % 128, 1)
                    for target, value, spot in (
                        (q - 1, outer, 2 * k + 1),
                        (q + 4 + 1, outer, 2 * k),
                        (q + 4 - 1, inner, 2 * k + 1),
                        (q + 1, inner, 2 * k),
                    ):
                        if 0 <= target < 8:
                            edge_ref[target] = jnp.where(lane == spot, value, edge_ref[target])
    for g in range(8):
        out_ref[pl.ds(g * out_rows + out_rows - 1, 32, stride=8 * out_rows), :] = edge_ref[g]


vmem = pl.BlockSpec(memory_space=pltpu.VMEM)
params = pltpu.CompilerParams(vmem_limit_bytes=24 * 2**20)


def solve_lines(own, other, weights, fields):
    return pl.pallas_call(
        functools.partial(solve_kernel, fields),
        out_shape=jax.ShapeDtypeStruct((own.shape[0] + 256, 128), jnp.float32),
        in_specs=[vmem] * 6,
        out_specs=vmem,
        scratch_shapes=[pltpu.VMEM((fields * 128, 512), jnp.float32), pltpu.VMEM((8, 32, 128), jnp.float32)],
        compiler_params=params,
        cost_estimate=pl.CostEstimate(
            flops=fields * 128 * 512 * (512 + 256) * 6, bytes_accessed=8 * 2**20, transcendentals=0
        ),
    )(own, other, *weights)


def weights_kernel(wz_ref, ix_ref, wz_high, wz_low, ix_high, ix_low):
    wz_high[...], wz_low[...] = parts(wz_ref[...])
    for yy in range(4):
        for zh in range(2):
            j = zh * 4 + yy
            rows = jnp.concatenate([ix_ref[q, pl.ds(64 * j, 64), :] for q in range(4)], axis=1)
            at = pl.ds(64 * (2 * yy + zh), 64)
            ix_high[at, :], ix_low[at, :] = parts(rows)


def prepared(wz, ix):
    half = lambda shape: jax.ShapeDtypeStruct(shape, jnp.bfloat16)
    count = ix.shape[1]
    return pl.pallas_call(
        weights_kernel,
        out_shape=(half(wz.shape), half(wz.shape), half((count, count)), half((count, count))),
        in_specs=[vmem] * 2,
        out_specs=(vmem,) * 4,
        compiler_params=params,
        cost_estimate=pl.CostEstimate(flops=2**20, bytes_accessed=2 * 2**20, transcendentals=0),
    )(wz, ix)


def masked_kernel(fields, got_ref, mask_ref, masked_ref, low_ref, high_ref, edge_ref):
    rows = got_ref.shape[0] // 256
    for c in range(fields):
        for pair in range(2):
            both = got_ref[pl.ds(2 * c + pair, 256, stride=rows), :].T
            for i in range(2):
                z = 2 * pair + i
                cells = both[64 * i : 64 * i + 64] * mask_ref[z]
                masked_ref[c, z] = cells
                if z == 0:
                    low_ref[c] = cells
                if z == 3:
                    high_ref[c] = cells
    edge_ref[...] = got_ref[pl.ds(rows - 1, 256, stride=rows), :].T[: 8 * fields]


def masked_cells(got, mask, fields):
    z_rows, x_rows, y_cells = mask.shape
    cells = lambda *shape: jax.ShapeDtypeStruct(shape, jnp.float32)
    return pl.pallas_call(
        functools.partial(masked_kernel, fields),
        out_shape=(
            cells(fields, z_rows, x_rows, y_cells),
            cells(fields, x_rows, y_cells),
            cells(fields, x_rows, y_cells),
            cells(2 * fields * z_rows, y_cells),
        ),
        in_specs=[vmem] * 2,
        out_specs=(vmem,) * 4,
        compiler_params=params,
        cost_estimate=pl.CostEstimate(flops=2**20, bytes_accessed=3 * 2**20, transcendentals=0),
    )(got, mask)


def stencil_kernel(fields, masked_ref, edge_ref, rim_ref, below_ref, above_ref, flow_ref, thick_ref, out_ref):
    row = lax.broadcasted_iota(jnp.int32, (64, 256), 0)
    lane = lax.broadcasted_iota(jnp.int32, (64, 256), 1)
    for z in range(4):
        flow_x, flow_z, flow_y = (flow_ref[i, z] for i in range(3))
        thick = thick_ref[z]
        for c in range(fields):
            k = 2 * (c * 4 + z)
            v = masked_ref[c, z]
            first = edge_ref[k : k + 1, :] * rim_ref[z : z + 1, :]
            last = edge_ref[k + 1 : k + 2, :] * rim_ref[4 + z : 5 + z, :]
            x_less = jnp.where(row == 0, first, pltpu.roll(v, 1, 0))
            x_more = jnp.where(row == 63, last, pltpu.roll(v, 63, 0))
            y_less = jnp.where(lane == 0, 0.0, pltpu.roll(v, 1, 1))
            y_more = jnp.where(lane == 255, 0.0, pltpu.roll(v, 255, 1))
            z_less = below_ref[c] if z == 0 else masked_ref[c, z - 1]
            z_more = above_ref[c] if z == 3 else masked_ref[c, z + 1]
            laplace = x_more + x_less + z_more + z_less + y_more + y_less - 6.0 * v
            slopes = flow_x * (x_more - x_less) + flow_z * (z_more - z_less) + flow_y * (y_more - y_less)
            done = v + time_step * (0.5 * slopes + thick * laplace)
            for half in range(2):
                out_ref[pl.ds(c * 512 + half * 4 + z, 64, stride=8), :] = done[:, half * 128 : half * 128 + 128]


def stencil(masked, edges, rim, below, above, flow, thick):
    fields, z_rows, x_rows, y_cells = masked.shape
    out = pl.pallas_call(
        functools.partial(stencil_kernel, fields),
        out_shape=jax.ShapeDtypeStruct((fields * x_rows * z_rows * y_cells // 128, 128), jnp.float32),
        in_specs=[vmem] * 7,
        out_specs=vmem,
        compiler_params=params,
        cost_estimate=pl.CostEstimate(flops=2**23, bytes_accessed=5 * 2**20, transcendentals=0),
    )(masked, edges, rim, below, above, flow, thick)
    out = out.reshape(fields, x_rows, y_cells // 128, z_rows, 128)
    return out.transpose(0, 1, 3, 2, 4).reshape(fields, x_rows, z_rows, y_cells)


def before_and_after(head, tail, axes):
    count = lax.axis_size(axes)
    before = lax.ppermute(tail, axes, [(i, i + 1) for i in range(count - 1)])
    after = lax.ppermute(head, axes, [(i + 1, i) for i in range(count - 1)])
    return before, after


def transposed(sent):
    return lax.all_to_all(sent, chips, split_axis=0, concat_axis=0, tiled=True)


def body(
    adj_out,
    advect,
    viscosity,
    body_mask,
    marker_x,
    marker_z,
    marker_y,
    drag_weight,
    inv_x,
    inv_y,
    inv_z,
):
    fields, x_rows, z_rows, y_cells = adj_out.shape
    pair = inv_x_pair(inv_x)
    wz = z_weights(inv_z, z_rows)
    pushed = pushes(marker_x, marker_z, marker_y, drag_weight, x_rows, z_rows, y_cells)
    seeded = adj_out.at[0].add(pushed)
    ysolved = jnp.einsum("lm,cxzl->mczx", inv_y, seeded, precision=highest)
    pair, sent = lax.optimization_barrier((pair, ysolved.reshape(y_cells, fields * z_rows * x_rows)))
    got = transposed(sent).reshape(-1, 128)
    full_x = whole_inv_x(pair)
    weights = prepared(wz, full_x)
    mask = body_mask.astype(jnp.float32).transpose(1, 0, 2)
    rim = jnp.concatenate(before_and_after(mask[:, 0], mask[:, -1], grp), axis=0)
    flow = advect.astype(jnp.float32).transpose(0, 2, 1, 3)
    thick = viscosity.astype(jnp.float32).transpose(1, 0, 2)
    other = lax.ppermute(got, "co", swap)
    back = solve_lines(got, other, weights, fields)
    solved = transposed(back.reshape(y_cells, -1)).reshape(-1, 128)
    masked, low, high, edges = masked_cells(solved, mask, fields)
    below, above = before_and_after(low, high, slab)
    return stencil(masked, edges, rim, below, above, flow, thick)


def solution(mesh):
    fine = Mesh(mesh.devices.reshape(8, 4, 2, 2, 4), ("zl", "xx", "co", "zh", "yy"))
    field = P(None, grp, slab, None)
    in_specs = (field, field, P(grp, slab, None), P(grp, slab, None), P(), P(), P(), P(), P(None, grp), P(), P())

    return jax.shard_map(body, mesh=fine, in_specs=in_specs, out_specs=field, check_vma=False)
```

```python
import functools

import jax
import jax.numpy as jnp
from jax import lax
from jax.experimental import pallas as pl
from jax.experimental.pallas import tpu as pltpu
from jax.sharding import Mesh, PartitionSpec as P


time_step = 0.08
highest = lax.Precision.HIGHEST
chips = ("zl", "xx", "zh", "yy")
slab = ("zl", "xx", "co")
grp = ("zh", "yy")
swap = [(0, 1), (1, 0)]


def parts(value):
    high = value.astype(jnp.bfloat16)
    return high, (value - high.astype(jnp.float32)).astype(jnp.bfloat16)


def product(left, right):
    dot = functools.partial(jnp.dot, preferred_element_type=jnp.float32)
    return dot(left[0], right[0]) + (dot(left[0], right[1]) + dot(left[1], right[0]))


def gather_ring(block, axis):
    count = lax.axis_size(axis)
    me = lax.axis_index(axis)
    out = jnp.zeros((count,) + block.shape, block.dtype)
    out = lax.dynamic_update_index_in_dim(out, block, me, 0)
    for hop in range(1, count):
        from_it = lax.ppermute(block, axis, [(i, (i + hop) % count) for i in range(count)])
        out = lax.dynamic_update_index_in_dim(out, from_it, (me - hop) % count, 0)
    return out


def inv_x_pair(inv_x):
    pieces = lax.axis_size("xx") * lax.axis_size("co")
    depth = inv_x.shape[0] // pieces
    mine = lax.dynamic_slice_in_dim(inv_x, lax.axis_index(("xx", "co")) * depth, depth, axis=0)
    theirs = lax.ppermute(mine, "zh", swap)
    low = lax.axis_index("zh") == 0
    return jnp.concatenate([jnp.where(low, mine, theirs), jnp.where(low, theirs, mine)], axis=1)


def whole_inv_x(pair):
    for axis in ("co", "xx", "yy"):
        pair = gather_ring(pair, axis)
    return pair.reshape(pair.shape[0], -1, pair.shape[-1])


def z_of(k, which, half, z_rows):
    groups = half // z_rows
    return (k % groups) * (2 * z_rows) + which * z_rows + k // groups


def push_plane(marker_x, marker_z, marker_y, drag_weight, inv_y, x_rows, z_rows):
    y_cells = inv_y.shape[0]
    core = lax.axis_index("co")
    y_mine = lax.axis_index(chips)
    to_y = lax.dynamic_slice_in_dim(inv_y, y_mine, 1, axis=1)
    at_y = marker_y[:, None] == lax.broadcasted_iota(jnp.int32, (1, y_cells), 1)
    amount = drag_weight * jnp.dot(at_y.astype(jnp.float32), to_y, precision=highest)[:, 0]
    z_count = 2 * lax.axis_size("zl") * lax.axis_size("xx") * z_rows
    row = lax.broadcasted_iota(jnp.int32, (z_count, 1), 0)
    half = z_count // 2
    z_row = jnp.where(row < half, z_of(row, core, half, z_rows), z_of(row - half, 1 - core, half, z_rows))
    y_size, h_size = lax.axis_size("yy"), lax.axis_size("zh")
    lane = lax.broadcasted_iota(jnp.int32, (1, y_size * h_size * x_rows), 1)
    block = lane // x_rows
    x_lane = ((block % h_size) * y_size + block // h_size) * x_rows + lane % x_rows
    at_z = (z_row == marker_z[None, :]).astype(jnp.float32)
    at_x = jnp.where(marker_x[:, None] == x_lane, amount[:, None], 0.0)
    return jnp.dot(at_z, at_x, precision=highest)


def z_weights(inv_z, z_rows):
    count = inv_z.shape[0]
    half = count // 2
    core = lax.axis_index("co")

    def chosen(which):
        k = lax.broadcasted_iota(jnp.int32, (half, count), 0)
        z = lax.broadcasted_iota(jnp.int32, (half, count), 1)
        return (z == z_of(k, which, half, z_rows)).astype(jnp.float32)

    mine = chosen(core)
    both = jnp.concatenate([mine, chosen(1 - core)], axis=0)
    picked = jnp.einsum("az,zw->aw", both, inv_z, precision=highest)
    return jnp.einsum("bw,aw->ba", mine, picked, precision=highest)


def solve_kernel(fields, own_ref, other_ref, push_ref, wz_high, wz_low, ix_high, ix_low, out_ref, z_ref, edge_ref):
    rows = own_ref.shape[0] // 256
    out_rows = out_ref.shape[0] // 256
    lane = lax.broadcasted_iota(jnp.int32, (32, 128), 1)
    low_half = lane < 64

    def lines(ref, c):
        evens, odds = [None, None], [None, None]
        for pair in range(2):
            even, odd = [], []
            for q in range(4):
                at = q * rows + 2 * c + pair
                first = ref[pl.ds(at, 32, stride=8 * rows), :]
                second = ref[pl.ds(at + 4 * rows, 32, stride=8 * rows), :]
                even.append(jnp.where(low_half, first, pltpu.roll(second, 64, 1)))
                odd.append(jnp.where(low_half, pltpu.roll(first, 64, 1), second))
            evens[pair] = jnp.concatenate(even, axis=1)
            odds[pair] = jnp.concatenate(odd, axis=1)
        return jnp.concatenate([evens[0], odds[0], evens[1], odds[1]], axis=0)

    wz = wz_high[...], wz_low[...]
    for c in range(fields):
        both = jnp.concatenate([lines(own_ref, c), lines(other_ref, c)], axis=0)
        if c == 0:
            both = both + push_ref[...]
        z_ref[pl.ds(c * 128, 128), :] = product(wz, parts(both))
    ix = ix_high[...], ix_low[...]
    edge_ref[...] = jnp.zeros_like(edge_ref)
    for c in range(fields):
        done = product(parts(z_ref[pl.ds(c * 128, 128), :]), ix)
        for pair in range(2):
            for q in range(4):
                two = [done[(2 * pair + i) * 32 : (2 * pair + i + 1) * 32, q * 128 : q * 128 + 128] for i in range(2)]
                at = q * out_rows + 2 * c + pair
                first = jnp.where(low_half, two[0], pltpu.roll(two[1], 64, 1))
                second = jnp.where(low_half, pltpu.roll(two[0], 64, 1), two[1])
                out_ref[pl.ds(at, 32, stride=8 * out_rows), :] = first
                out_ref[pl.ds(at + 4 * out_rows, 32, stride=8 * out_rows), :] = second
                for i in range(2):
                    k = c * 4 + 2 * pair + i
                    outer = pltpu.roll(two[i], 2 * k + 1, 1)
                    inner = pltpu.roll(two[i], (2 * k + 65) % 128, 1)
                    for target, value, spot in (
                        (q - 1, outer, 2 * k + 1),
                        (q + 4 + 1, outer, 2 * k),
                        (q + 4 - 1, inner, 2 * k + 1),
                        (q + 1, inner, 2 * k),
                    ):
                        if 0 <= target < 8:
                            edge_ref[target] = jnp.where(lane == spot, value, edge_ref[target])
    for g in range(8):
        out_ref[pl.ds(g * out_rows + out_rows - 1, 32, stride=8 * out_rows), :] = edge_ref[g]


vmem = pl.BlockSpec(memory_space=pltpu.VMEM)
params = pltpu.CompilerParams(vmem_limit_bytes=24 * 2**20)


def solve_lines(own, other, push, weights, fields):
    return pl.pallas_call(
        functools.partial(solve_kernel, fields),
        out_shape=jax.ShapeDtypeStruct((own.shape[0] + 256, 128), jnp.float32),
        in_specs=[vmem] * 7,
        out_specs=vmem,
        scratch_shapes=[pltpu.VMEM((fields * 128, 512), jnp.float32), pltpu.VMEM((8, 32, 128), jnp.float32)],
        compiler_params=params,
        cost_estimate=pl.CostEstimate(
            flops=fields * 128 * 512 * (512 + 256) * 6, bytes_accessed=8 * 2**20, transcendentals=0
        ),
    )(own, other, push, *weights)


def y_kernel(fields, cells_ref, inv_ref, out_ref):
    inv = parts(inv_ref[...].T)
    rows = 2 * fields
    contract = (((1,), (1,)), ((), ()))
    dot = lambda a, b: lax.dot_general(a, b, contract, preferred_element_type=jnp.float32)
    for c in range(fields):
        for pair in range(2):
            both = []
            for z in (2 * pair, 2 * pair + 1):
                tiles = [cells_ref[pl.ds(c * 512 + 4 * tile + z, 64, stride=8), :] for tile in range(2)]
                both.append(jnp.concatenate(tiles, axis=1))
            high, low = parts(jnp.concatenate(both, axis=0))
            done = dot(inv[0], high) + (dot(inv[0], low) + dot(inv[1], high))
            out_ref[pl.ds(2 * c + pair, 256, stride=rows), :] = done


def y_solved(cells, inv_y):
    fields, x_rows, z_rows, y_cells = cells.shape
    tiles = cells.reshape(fields, x_rows, z_rows, y_cells // 128, 128).transpose(0, 1, 3, 2, 4).reshape(-1, 128)
    return pl.pallas_call(
        functools.partial(y_kernel, fields),
        out_shape=jax.ShapeDtypeStruct(tiles.shape, jnp.float32),
        in_specs=[vmem] * 2,
        out_specs=vmem,
        compiler_params=params,
        cost_estimate=pl.CostEstimate(flops=6 * tiles.size * y_cells, bytes_accessed=3 * 2**20, transcendentals=0),
    )(tiles, inv_y)


def weights_kernel(wz_ref, ix_ref, wz_high, wz_low, ix_high, ix_low):
    wz_high[...], wz_low[...] = parts(wz_ref[...])
    for yy in range(4):
        for zh in range(2):
            j = zh * 4 + yy
            rows = jnp.concatenate([ix_ref[q, pl.ds(64 * j, 64), :] for q in range(4)], axis=1)
            at = pl.ds(64 * (2 * yy + zh), 64)
            ix_high[at, :], ix_low[at, :] = parts(rows)


def prepared(wz, ix):
    half = lambda shape: jax.ShapeDtypeStruct(shape, jnp.bfloat16)
    count = ix.shape[1]
    return pl.pallas_call(
        weights_kernel,
        out_shape=(half(wz.shape), half(wz.shape), half((count, count)), half((count, count))),
        in_specs=[vmem] * 2,
        out_specs=(vmem,) * 4,
        compiler_params=params,
        cost_estimate=pl.CostEstimate(flops=2**20, bytes_accessed=2 * 2**20, transcendentals=0),
    )(wz, ix)


def masked_kernel(fields, got_ref, mask_ref, masked_ref, low_ref, high_ref, edge_ref):
    rows = got_ref.shape[0] // 256
    for c in range(fields):
        for pair in range(2):
            both = got_ref[pl.ds(2 * c + pair, 256, stride=rows), :].T
            for i in range(2):
                z = 2 * pair + i
                cells = both[64 * i : 64 * i + 64] * mask_ref[z]
                masked_ref[c, z] = cells
                if z == 0:
                    low_ref[c] = cells
                if z == 3:
                    high_ref[c] = cells
    edge_ref[...] = got_ref[pl.ds(rows - 1, 256, stride=rows), :].T[: 8 * fields]


def masked_cells(got, mask, fields):
    z_rows, x_rows, y_cells = mask.shape
    cells = lambda *shape: jax.ShapeDtypeStruct(shape, jnp.float32)
    return pl.pallas_call(
        functools.partial(masked_kernel, fields),
        out_shape=(
            cells(fields, z_rows, x_rows, y_cells),
            cells(fields, x_rows, y_cells),
            cells(fields, x_rows, y_cells),
            cells(2 * fields * z_rows, y_cells),
        ),
        in_specs=[vmem] * 2,
        out_specs=(vmem,) * 4,
        compiler_params=params,
        cost_estimate=pl.CostEstimate(flops=2**20, bytes_accessed=3 * 2**20, transcendentals=0),
    )(got, mask)


def stencil_kernel(fields, masked_ref, edge_ref, rim_ref, below_ref, above_ref, flow_ref, thick_ref, out_ref):
    row = lax.broadcasted_iota(jnp.int32, (64, 256), 0)
    lane = lax.broadcasted_iota(jnp.int32, (64, 256), 1)
    for z in range(4):
        flow_x, flow_z, flow_y = (flow_ref[i, z] for i in range(3))
        thick = thick_ref[z]
        for c in range(fields):
            k = 2 * (c * 4 + z)
            v = masked_ref[c, z]
            first = edge_ref[k : k + 1, :] * rim_ref[z : z + 1, :]
            last = edge_ref[k + 1 : k + 2, :] * rim_ref[4 + z : 5 + z, :]
            x_less = jnp.where(row == 0, first, pltpu.roll(v, 1, 0))
            x_more = jnp.where(row == 63, last, pltpu.roll(v, 63, 0))
            y_less = jnp.where(lane == 0, 0.0, pltpu.roll(v, 1, 1))
            y_more = jnp.where(lane == 255, 0.0, pltpu.roll(v, 255, 1))
            z_less = below_ref[c] if z == 0 else masked_ref[c, z - 1]
            z_more = above_ref[c] if z == 3 else masked_ref[c, z + 1]
            laplace = x_more + x_less + z_more + z_less + y_more + y_less - 6.0 * v
            slopes = flow_x * (x_more - x_less) + flow_z * (z_more - z_less) + flow_y * (y_more - y_less)
            done = v + time_step * (0.5 * slopes + thick * laplace)
            for half in range(2):
                out_ref[pl.ds(c * 512 + half * 4 + z, 64, stride=8), :] = done[:, half * 128 : half * 128 + 128]


def stencil(masked, edges, rim, below, above, flow, thick):
    fields, z_rows, x_rows, y_cells = masked.shape
    out = pl.pallas_call(
        functools.partial(stencil_kernel, fields),
        out_shape=jax.ShapeDtypeStruct((fields * x_rows * z_rows * y_cells // 128, 128), jnp.float32),
        in_specs=[vmem] * 7,
        out_specs=vmem,
        compiler_params=params,
        cost_estimate=pl.CostEstimate(flops=2**23, bytes_accessed=5 * 2**20, transcendentals=0),
    )(masked, edges, rim, below, above, flow, thick)
    out = out.reshape(fields, x_rows, y_cells // 128, z_rows, 128)
    return out.transpose(0, 1, 3, 2, 4).reshape(fields, x_rows, z_rows, y_cells)


def before_and_after(head, tail, axes):
    count = lax.axis_size(axes)
    before = lax.ppermute(tail, axes, [(i, i + 1) for i in range(count - 1)])
    after = lax.ppermute(head, axes, [(i + 1, i) for i in range(count - 1)])
    return before, after


def transposed(sent):
    return lax.all_to_all(sent, chips, split_axis=0, concat_axis=0, tiled=True)


def body(
    adj_out,
    advect,
    viscosity,
    body_mask,
    marker_x,
    marker_z,
    marker_y,
    drag_weight,
    inv_x,
    inv_y,
    inv_z,
):
    fields, x_rows, z_rows, y_cells = adj_out.shape
    pair = inv_x_pair(inv_x)
    wz = z_weights(inv_z, z_rows)
    sent = y_solved(adj_out, inv_y).reshape(y_cells, -1)
    got = transposed(sent).reshape(-1, 128)
    push = push_plane(marker_x, marker_z, marker_y, drag_weight, inv_y, x_rows, z_rows)
    full_x = whole_inv_x(pair)
    weights = prepared(wz, full_x)
    mask = body_mask.astype(jnp.float32).transpose(1, 0, 2)
    rim = jnp.concatenate(before_and_after(mask[:, 0], mask[:, -1], grp), axis=0)
    flow = advect.astype(jnp.float32).transpose(0, 2, 1, 3)
    thick = viscosity.astype(jnp.float32).transpose(1, 0, 2)
    other = lax.ppermute(got, "co", swap)
    back = solve_lines(got, other, push, weights, fields)
    solved = transposed(back.reshape(y_cells, -1)).reshape(-1, 128)
    masked, low, high, edges = masked_cells(solved, mask, fields)
    below, above = before_and_after(low, high, slab)
    return stencil(masked, edges, rim, below, above, flow, thick)


def solution(mesh):
    fine = Mesh(mesh.devices.reshape(8, 4, 2, 2, 4), ("zl", "xx", "co", "zh", "yy"))
    field = P(None, grp, slab, None)
    in_specs = (field, field, P(grp, slab, None), P(grp, slab, None), P(), P(), P(), P(), P(None, grp), P(), P())

    return jax.shard_map(body, mesh=fine, in_specs=in_specs, out_specs=field, check_vma=False)
```

```python
import functools

import jax
import jax.numpy as jnp
from jax import lax
from jax.experimental import pallas as pl
from jax.experimental.pallas import tpu as pltpu
from jax.sharding import Mesh, PartitionSpec as P


time_step = 0.08
highest = lax.Precision.HIGHEST
chips = ("zl", "xx", "zh", "yy")
slab = ("zl", "xx", "co")
grp = ("zh", "yy")
swap = [(0, 1), (1, 0)]


def parts(value):
    high = value.astype(jnp.bfloat16)
    return high, (value - high.astype(jnp.float32)).astype(jnp.bfloat16)


def product(left, right):
    dot = functools.partial(jnp.dot, preferred_element_type=jnp.float32)
    return dot(left[0], right[0]) + (dot(left[0], right[1]) + dot(left[1], right[0]))


def gather_ring(block, axis):
    count = lax.axis_size(axis)
    me = lax.axis_index(axis)
    out = jnp.zeros((count,) + block.shape, block.dtype)
    out = lax.dynamic_update_index_in_dim(out, block, me, 0)
    for hop in range(1, count):
        from_it = lax.ppermute(block, axis, [(i, (i + hop) % count) for i in range(count)])
        out = lax.dynamic_update_index_in_dim(out, from_it, (me - hop) % count, 0)
    return out


def inv_x_pair(inv_x):
    pieces = lax.axis_size("xx") * lax.axis_size("co")
    depth = inv_x.shape[0] // pieces
    mine = lax.dynamic_slice_in_dim(inv_x, lax.axis_index(("xx", "co")) * depth, depth, axis=0)
    theirs = lax.ppermute(mine, "zh", swap)
    low = lax.axis_index("zh") == 0
    return jnp.concatenate([jnp.where(low, mine, theirs), jnp.where(low, theirs, mine)], axis=1)


def whole_inv_x(pair):
    for axis in ("co", "xx", "yy"):
        pair = gather_ring(pair, axis)
    return pair.reshape(pair.shape[0], -1, pair.shape[-1])


def z_of(k, which, half, z_rows):
    groups = half // z_rows
    return (k % groups) * (2 * z_rows) + which * z_rows + k // groups


def push_plane(marker_x, marker_z, marker_y, drag_weight, inv_y, x_rows, z_rows):
    y_cells = inv_y.shape[0]
    core = lax.axis_index("co")
    y_mine = lax.axis_index(chips)
    to_y = lax.dynamic_slice_in_dim(inv_y, y_mine, 1, axis=1)
    at_y = marker_y[:, None] == lax.broadcasted_iota(jnp.int32, (1, y_cells), 1)
    amount = drag_weight * jnp.dot(at_y.astype(jnp.float32), to_y, precision=highest)[:, 0]
    z_count = 2 * lax.axis_size("zl") * lax.axis_size("xx") * z_rows
    row = lax.broadcasted_iota(jnp.int32, (z_count, 1), 0)
    half = z_count // 2
    z_row = jnp.where(row < half, z_of(row, core, half, z_rows), z_of(row - half, 1 - core, half, z_rows))
    y_size, h_size = lax.axis_size("yy"), lax.axis_size("zh")
    lane = lax.broadcasted_iota(jnp.int32, (1, y_size * h_size * x_rows), 1)
    block = lane // x_rows
    x_lane = ((block % h_size) * y_size + block // h_size) * x_rows + lane % x_rows
    at_z = (z_row == marker_z[None, :]).astype(jnp.float32)
    at_x = jnp.where(marker_x[:, None] == x_lane, amount[:, None], 0.0)
    return jnp.dot(at_z, at_x, precision=highest)


def z_weights(inv_z, z_rows):
    count = inv_z.shape[0]
    half = count // 2
    core = lax.axis_index("co")

    def chosen(which):
        k = lax.broadcasted_iota(jnp.int32, (half, count), 0)
        z = lax.broadcasted_iota(jnp.int32, (half, count), 1)
        return (z == z_of(k, which, half, z_rows)).astype(jnp.float32)

    mine = chosen(core)
    both = jnp.concatenate([mine, chosen(1 - core)], axis=0)
    picked = jnp.einsum("az,zw->aw", both, inv_z, precision=highest)
    return jnp.einsum("bw,aw->ba", mine, picked, precision=highest)


def solve_kernel(fields, own_ref, other_ref, push_ref, wz_high, wz_low, ix_high, ix_low, out_ref, z_ref, edge_ref):
    rows = own_ref.shape[0] // 256
    out_rows = out_ref.shape[0] // 256
    lane = lax.broadcasted_iota(jnp.int32, (32, 128), 1)
    low_half = lane < 64

    def lines(ref, c):
        evens, odds = [None, None], [None, None]
        for pair in range(2):
            even, odd = [], []
            for q in range(4):
                at = q * rows + 2 * c + pair
                first = ref[pl.ds(at, 32, stride=8 * rows), :]
                second = ref[pl.ds(at + 4 * rows, 32, stride=8 * rows), :]
                even.append(jnp.where(low_half, first, pltpu.roll(second, 64, 1)))
                odd.append(jnp.where(low_half, pltpu.roll(first, 64, 1), second))
            evens[pair] = jnp.concatenate(even, axis=1)
            odds[pair] = jnp.concatenate(odd, axis=1)
        return jnp.concatenate([evens[0], odds[0], evens[1], odds[1]], axis=0)

    wz = wz_high[...], wz_low[...]
    for c in range(fields):
        both = jnp.concatenate([lines(own_ref, c), lines(other_ref, c)], axis=0)
        if c == 0:
            both = both + push_ref[...]
        z_ref[pl.ds(c * 128, 128), :] = product(wz, parts(both))
    ix = ix_high[...], ix_low[...]
    edge_ref[...] = jnp.zeros_like(edge_ref)
    for c in range(fields):
        done = product(parts(z_ref[pl.ds(c * 128, 128), :]), ix)
        for pair in range(2):
            for q in range(4):
                two = [done[(2 * pair + i) * 32 : (2 * pair + i + 1) * 32, q * 128 : q * 128 + 128] for i in range(2)]
                at = q * out_rows + 2 * c + pair
                first = jnp.where(low_half, two[0], pltpu.roll(two[1], 64, 1))
                second = jnp.where(low_half, pltpu.roll(two[0], 64, 1), two[1])
                out_ref[pl.ds(at, 32, stride=8 * out_rows), :] = first
                out_ref[pl.ds(at + 4 * out_rows, 32, stride=8 * out_rows), :] = second
                for i in range(2):
                    k = c * 4 + 2 * pair + i
                    outer = pltpu.roll(two[i], 2 * k + 1, 1)
                    inner = pltpu.roll(two[i], (2 * k + 65) % 128, 1)
                    for target, value, spot in (
                        (q - 1, outer, 2 * k + 1),
                        (q + 4 + 1, outer, 2 * k),
                        (q + 4 - 1, inner, 2 * k + 1),
                        (q + 1, inner, 2 * k),
                    ):
                        if 0 <= target < 8:
                            edge_ref[target] = jnp.where(lane == spot, value, edge_ref[target])
    for g in range(8):
        out_ref[pl.ds(g * out_rows + out_rows - 1, 32, stride=8 * out_rows), :] = edge_ref[g]


vmem = pl.BlockSpec(memory_space=pltpu.VMEM)
params = pltpu.CompilerParams(vmem_limit_bytes=24 * 2**20)


def solve_lines(own, other, push, weights, fields):
    return pl.pallas_call(
        functools.partial(solve_kernel, fields),
        out_shape=jax.ShapeDtypeStruct((own.shape[0] + 256, 128), jnp.float32),
        in_specs=[vmem] * 7,
        out_specs=vmem,
        scratch_shapes=[pltpu.VMEM((fields * 128, 512), jnp.float32), pltpu.VMEM((8, 32, 128), jnp.float32)],
        compiler_params=params,
        cost_estimate=pl.CostEstimate(
            flops=fields * 128 * 512 * (512 + 256) * 6, bytes_accessed=8 * 2**20, transcendentals=0
        ),
    )(own, other, push, *weights)


def y_kernel(fields, cells_ref, inv_ref, out_ref, high_ref, low_ref):
    c = pl.program_id(0)

    @pl.when(c == 0)
    def _():
        high_ref[...], low_ref[...] = parts(inv_ref[...].T)

    contract = (((1,), (1,)), ((), ()))
    dot = lambda a, b: lax.dot_general(a, b, contract, preferred_element_type=jnp.float32)
    for pair in range(2):
        both = []
        for z in (2 * pair, 2 * pair + 1):
            tiles = [cells_ref[pl.ds(4 * tile + z, 64, stride=8), :] for tile in range(2)]
            both.append(jnp.concatenate(tiles, axis=1))
        high, low = parts(jnp.concatenate(both, axis=0))
        done = dot(high_ref[...], high) + (dot(high_ref[...], low) + dot(low_ref[...], high))
        out_ref[pl.ds(2 * c + pair, 256, stride=2 * fields), :] = done


def y_solved(cells, inv_y):
    fields, x_rows, z_rows, y_cells = cells.shape
    tiles = cells.reshape(fields, x_rows, z_rows, y_cells // 128, 128).transpose(0, 1, 3, 2, 4).reshape(-1, 128)
    return pl.pallas_call(
        functools.partial(y_kernel, fields),
        grid=(fields,),
        out_shape=jax.ShapeDtypeStruct(tiles.shape, jnp.float32),
        in_specs=[
            pl.BlockSpec((tiles.shape[0] // fields, 128), lambda c: (c, 0)),
            pl.BlockSpec(inv_y.shape, lambda c: (0, 0)),
        ],
        out_specs=pl.BlockSpec(tiles.shape, lambda c: (0, 0)),
        scratch_shapes=[pltpu.VMEM(inv_y.shape, jnp.bfloat16)] * 2,
        compiler_params=pltpu.CompilerParams(vmem_limit_bytes=61000 * 1024),
        cost_estimate=pl.CostEstimate(flops=6 * tiles.size * y_cells, bytes_accessed=3 * 2**20, transcendentals=0),
    )(tiles, inv_y)


def weights_kernel(wz_ref, ix_ref, wz_high, wz_low, ix_high, ix_low):
    wz_high[...], wz_low[...] = parts(wz_ref[...])
    for yy in range(4):
        for zh in range(2):
            j = zh * 4 + yy
            rows = jnp.concatenate([ix_ref[q, pl.ds(64 * j, 64), :] for q in range(4)], axis=1)
            at = pl.ds(64 * (2 * yy + zh), 64)
            ix_high[at, :], ix_low[at, :] = parts(rows)


def prepared(wz, ix):
    half = lambda shape: jax.ShapeDtypeStruct(shape, jnp.bfloat16)
    count = ix.shape[1]
    return pl.pallas_call(
        weights_kernel,
        out_shape=(half(wz.shape), half(wz.shape), half((count, count)), half((count, count))),
        in_specs=[vmem] * 2,
        out_specs=(vmem,) * 4,
        compiler_params=params,
        cost_estimate=pl.CostEstimate(flops=2**20, bytes_accessed=2 * 2**20, transcendentals=0),
    )(wz, ix)


def masked_kernel(fields, got_ref, mask_ref, masked_ref, low_ref, high_ref, edge_ref):
    rows = got_ref.shape[0] // 256
    for c in range(fields):
        for pair in range(2):
            both = got_ref[pl.ds(2 * c + pair, 256, stride=rows), :].T
            for i in range(2):
                z = 2 * pair + i
                cells = both[64 * i : 64 * i + 64] * mask_ref[z]
                masked_ref[c, z] = cells
                if z == 0:
                    low_ref[c] = cells
                if z == 3:
                    high_ref[c] = cells
    edge_ref[...] = got_ref[pl.ds(rows - 1, 256, stride=rows), :].T[: 8 * fields]


def masked_cells(got, mask, fields):
    z_rows, x_rows, y_cells = mask.shape
    cells = lambda *shape: jax.ShapeDtypeStruct(shape, jnp.float32)
    return pl.pallas_call(
        functools.partial(masked_kernel, fields),
        out_shape=(
            cells(fields, z_rows, x_rows, y_cells),
            cells(fields, x_rows, y_cells),
            cells(fields, x_rows, y_cells),
            cells(2 * fields * z_rows, y_cells),
        ),
        in_specs=[vmem] * 2,
        out_specs=(vmem,) * 4,
        compiler_params=params,
        cost_estimate=pl.CostEstimate(flops=2**20, bytes_accessed=3 * 2**20, transcendentals=0),
    )(got, mask)


def stencil_kernel(fields, masked_ref, edge_ref, rim_ref, flow_ref, thick_ref, out_ref):
    row = lax.broadcasted_iota(jnp.int32, (64, 256), 0)
    lane = lax.broadcasted_iota(jnp.int32, (64, 256), 1)
    for z in range(4):
        flow_x, flow_z, flow_y = (flow_ref[i, z] for i in range(3))
        thick = thick_ref[z]
        for c in range(fields):
            k = 2 * (c * 4 + z)
            v = masked_ref[c, z]
            first = edge_ref[k : k + 1, :] * rim_ref[z : z + 1, :]
            last = edge_ref[k + 1 : k + 2, :] * rim_ref[4 + z : 5 + z, :]
            x_less = jnp.where(row == 0, first, pltpu.roll(v, 1, 0))
            x_more = jnp.where(row == 63, last, pltpu.roll(v, 63, 0))
            y_less = jnp.where(lane == 0, 0.0, pltpu.roll(v, 1, 1))
            y_more = jnp.where(lane == 255, 0.0, pltpu.roll(v, 255, 1))
            around = x_more + x_less + y_more + y_less - 6.0 * v
            slopes = flow_x * (x_more - x_less) + flow_y * (y_more - y_less)
            if z > 0:
                around, slopes = around + masked_ref[c, z - 1], slopes - flow_z * masked_ref[c, z - 1]
            if z < 3:
                around, slopes = around + masked_ref[c, z + 1], slopes + flow_z * masked_ref[c, z + 1]
            done = v + time_step * (0.5 * slopes + thick * around)
            for half in range(2):
                out_ref[pl.ds(c * 512 + half * 4 + z, 64, stride=8), :] = done[:, half * 128 : half * 128 + 128]


def rim_kernel(fields, most_ref, below_ref, above_ref, flow_ref, thick_ref, out_ref):
    low = time_step * (thick_ref[0] - 0.5 * flow_ref[1, 0])
    high = time_step * (thick_ref[3] + 0.5 * flow_ref[1, 3])
    for c in range(fields):
        for z in range(4):
            added = low * below_ref[c] if z == 0 else high * above_ref[c] if z == 3 else None
            for half in range(2):
                at = pl.ds(c * 512 + half * 4 + z, 64, stride=8)
                value = most_ref[at, :]
                out_ref[at, :] = value if added is None else value + added[:, half * 128 : half * 128 + 128]


def stencil(masked, edges, rim, below, above, flow, thick):
    fields, z_rows, x_rows, y_cells = masked.shape
    shape = jax.ShapeDtypeStruct((masked.size // 128, 128), jnp.float32)
    most = pl.pallas_call(
        functools.partial(stencil_kernel, fields),
        out_shape=shape,
        in_specs=[vmem] * 5,
        out_specs=vmem,
        compiler_params=params,
        cost_estimate=pl.CostEstimate(flops=2**23, bytes_accessed=5 * 2**20, transcendentals=0),
    )(masked, edges, rim, flow, thick)
    out = pl.pallas_call(
        functools.partial(rim_kernel, fields),
        out_shape=shape,
        in_specs=[vmem] * 5,
        out_specs=vmem,
        compiler_params=params,
        cost_estimate=pl.CostEstimate(flops=2**20, bytes_accessed=3 * 2**20, transcendentals=0),
    )(most, below, above, flow, thick)
    out = out.reshape(fields, x_rows, y_cells // 128, z_rows, 128)
    return out.transpose(0, 1, 3, 2, 4).reshape(fields, x_rows, z_rows, y_cells)


def before_and_after(head, tail, axes):
    count = lax.axis_size(axes)
    before = lax.ppermute(tail, axes, [(i, i + 1) for i in range(count - 1)])
    after = lax.ppermute(head, axes, [(i + 1, i) for i in range(count - 1)])
    return before, after


def transposed(sent):
    return lax.all_to_all(sent, chips, split_axis=0, concat_axis=0, tiled=True)


def body(
    adj_out,
    advect,
    viscosity,
    body_mask,
    marker_x,
    marker_z,
    marker_y,
    drag_weight,
    inv_x,
    inv_y,
    inv_z,
):
    fields, x_rows, z_rows, y_cells = adj_out.shape
    pair = inv_x_pair(inv_x)
    wz = z_weights(inv_z, z_rows)
    sent = y_solved(adj_out, inv_y).reshape(y_cells, -1)
    got = transposed(sent).reshape(-1, 128)
    push = push_plane(marker_x, marker_z, marker_y, drag_weight, inv_y, x_rows, z_rows)
    full_x = whole_inv_x(pair)
    weights = prepared(wz, full_x)
    mask = body_mask.astype(jnp.float32).transpose(1, 0, 2)
    rim = jnp.concatenate(before_and_after(mask[:, 0], mask[:, -1], grp), axis=0)
    flow = advect.astype(jnp.float32).transpose(0, 2, 1, 3)
    thick = viscosity.astype(jnp.float32).transpose(1, 0, 2)
    other = lax.ppermute(got, "co", swap)
    back = solve_lines(got, other, push, weights, fields)
    solved = transposed(back.reshape(y_cells, -1)).reshape(-1, 128)
    masked, low, high, edges = masked_cells(solved, mask, fields)
    below, above = before_and_after(low, high, slab)
    return stencil(masked, edges, rim, below, above, flow, thick)


def solution(mesh):
    fine = Mesh(mesh.devices.reshape(8, 4, 2, 2, 4), ("zl", "xx", "co", "zh", "yy"))
    field = P(None, grp, slab, None)
    in_specs = (field, field, P(grp, slab, None), P(grp, slab, None), P(), P(), P(), P(), P(None, grp), P(), P())

    return jax.shard_map(body, mesh=fine, in_specs=in_specs, out_specs=field, check_vma=False)
```

```python
import functools

import jax
import jax.numpy as jnp
from jax import lax
from jax.experimental import pallas as pl
from jax.experimental.pallas import tpu as pltpu
from jax.sharding import Mesh, PartitionSpec as P


time_step = 0.08
highest = lax.Precision.HIGHEST
chips = ("zl", "xx", "zh", "yy")
slab = ("zl", "xx", "co")
grp = ("zh", "yy")
swap = [(0, 1), (1, 0)]


def parts(value):
    high = value.astype(jnp.bfloat16)
    return high, (value - high.astype(jnp.float32)).astype(jnp.bfloat16)


def product(left, right):
    dot = functools.partial(jnp.dot, preferred_element_type=jnp.float32)
    return dot(left[0], right[0]) + (dot(left[0], right[1]) + dot(left[1], right[0]))


def gather_ring(block, axis):
    count = lax.axis_size(axis)
    me = lax.axis_index(axis)
    out = jnp.zeros((count,) + block.shape, block.dtype)
    out = lax.dynamic_update_index_in_dim(out, block, me, 0)
    for hop in range(1, count):
        from_it = lax.ppermute(block, axis, [(i, (i + hop) % count) for i in range(count)])
        out = lax.dynamic_update_index_in_dim(out, from_it, (me - hop) % count, 0)
    return out


def inv_x_pair(inv_x):
    pieces = lax.axis_size("xx") * lax.axis_size("co")
    depth = inv_x.shape[0] // pieces
    mine = lax.dynamic_slice_in_dim(inv_x, lax.axis_index(("xx", "co")) * depth, depth, axis=0)
    theirs = lax.ppermute(mine, "zh", swap)
    low = lax.axis_index("zh") == 0
    return jnp.concatenate([jnp.where(low, mine, theirs), jnp.where(low, theirs, mine)], axis=1)


def whole_inv_x(pair):
    for axis in ("xx", "yy", "co"):
        pair = gather_ring(pair, axis)
    return pair.reshape(*pair.shape[:2], -1, pair.shape[-1])


def z_of(k, which, half, z_rows):
    groups = half // z_rows
    return (k % groups) * (2 * z_rows) + which * z_rows + k // groups


def push_plane(marker_x, marker_z, marker_y, drag_weight, inv_y, x_rows, z_rows):
    y_cells = inv_y.shape[0]
    core = lax.axis_index("co")
    y_mine = lax.axis_index(chips)
    to_y = lax.dynamic_slice_in_dim(inv_y, y_mine, 1, axis=1)
    at_y = marker_y[:, None] == lax.broadcasted_iota(jnp.int32, (1, y_cells), 1)
    amount = drag_weight * jnp.dot(at_y.astype(jnp.float32), to_y, precision=highest)[:, 0]
    z_count = 2 * lax.axis_size("zl") * lax.axis_size("xx") * z_rows
    row = lax.broadcasted_iota(jnp.int32, (z_count, 1), 0)
    half = z_count // 2
    z_row = jnp.where(row < half, z_of(row, core, half, z_rows), z_of(row - half, 1 - core, half, z_rows))
    y_size, h_size = lax.axis_size("yy"), lax.axis_size("zh")
    lane = lax.broadcasted_iota(jnp.int32, (1, y_size * h_size * x_rows), 1)
    block = lane // x_rows
    x_lane = ((block % h_size) * y_size + block // h_size) * x_rows + lane % x_rows
    at_z = (z_row == marker_z[None, :]).astype(jnp.float32)
    at_x = jnp.where(marker_x[:, None] == x_lane, amount[:, None], 0.0)
    return jnp.dot(at_z, at_x, precision=highest)


def z_weights(inv_z, z_rows):
    count = inv_z.shape[0]
    half = count // 2
    core = lax.axis_index("co")

    def chosen(which):
        k = lax.broadcasted_iota(jnp.int32, (half, count), 0)
        z = lax.broadcasted_iota(jnp.int32, (half, count), 1)
        return (z == z_of(k, which, half, z_rows)).astype(jnp.float32)

    mine = chosen(core)
    both = jnp.concatenate([mine, chosen(1 - core)], axis=0)
    picked = jnp.einsum("az,zw->aw", both, inv_z, precision=highest)
    return jnp.einsum("bw,aw->ba", mine, picked, precision=highest)


def solve_kernel(fields, own_ref, other_ref, push_ref, wz_high, wz_low, ix_high, ix_low, out_ref, z_ref, edge_ref):
    rows = own_ref.shape[0] // 256
    out_rows = out_ref.shape[0] // 256
    lane = lax.broadcasted_iota(jnp.int32, (32, 128), 1)
    low_half = lane < 64

    def lines(ref, c):
        evens, odds = [None, None], [None, None]
        for pair in range(2):
            even, odd = [], []
            for q in range(4):
                at = q * rows + 2 * c + pair
                first = ref[pl.ds(at, 32, stride=8 * rows), :]
                second = ref[pl.ds(at + 4 * rows, 32, stride=8 * rows), :]
                even.append(jnp.where(low_half, first, pltpu.roll(second, 64, 1)))
                odd.append(jnp.where(low_half, pltpu.roll(first, 64, 1), second))
            evens[pair] = jnp.concatenate(even, axis=1)
            odds[pair] = jnp.concatenate(odd, axis=1)
        return jnp.concatenate([evens[0], odds[0], evens[1], odds[1]], axis=0)

    wz = wz_high[...], wz_low[...]
    for c in range(fields):
        both = jnp.concatenate([lines(own_ref, c), lines(other_ref, c)], axis=0)
        if c == 0:
            both = both + push_ref[...]
        z_ref[pl.ds(c * 128, 128), :] = product(wz, parts(both))
    ix = ix_high[...], ix_low[...]
    edge_ref[...] = jnp.zeros_like(edge_ref)
    for c in range(fields):
        done = product(parts(z_ref[pl.ds(c * 128, 128), :]), ix)
        for pair in range(2):
            for q in range(4):
                two = [done[(2 * pair + i) * 32 : (2 * pair + i + 1) * 32, q * 128 : q * 128 + 128] for i in range(2)]
                at = q * out_rows + 2 * c + pair
                first = jnp.where(low_half, two[0], pltpu.roll(two[1], 64, 1))
                second = jnp.where(low_half, pltpu.roll(two[0], 64, 1), two[1])
                out_ref[pl.ds(at, 32, stride=8 * out_rows), :] = first
                out_ref[pl.ds(at + 4 * out_rows, 32, stride=8 * out_rows), :] = second
                for i in range(2):
                    k = c * 4 + 2 * pair + i
                    outer = pltpu.roll(two[i], 2 * k + 1, 1)
                    inner = pltpu.roll(two[i], (2 * k + 65) % 128, 1)
                    for target, value, spot in (
                        (q - 1, outer, 2 * k + 1),
                        (q + 4 + 1, outer, 2 * k),
                        (q + 4 - 1, inner, 2 * k + 1),
                        (q + 1, inner, 2 * k),
                    ):
                        if 0 <= target < 8:
                            edge_ref[target] = jnp.where(lane == spot, value, edge_ref[target])
    for g in range(8):
        out_ref[pl.ds(g * out_rows + out_rows - 1, 32, stride=8 * out_rows), :] = edge_ref[g]


vmem = pl.BlockSpec(memory_space=pltpu.VMEM)
params = pltpu.CompilerParams(vmem_limit_bytes=24 * 2**20)


def solve_lines(own, other, push, weights, fields):
    return pl.pallas_call(
        functools.partial(solve_kernel, fields),
        out_shape=jax.ShapeDtypeStruct((own.shape[0] + 256, 128), jnp.float32),
        in_specs=[vmem] * 7,
        out_specs=vmem,
        scratch_shapes=[pltpu.VMEM((fields * 128, 512), jnp.float32), pltpu.VMEM((8, 32, 128), jnp.float32)],
        compiler_params=params,
        cost_estimate=pl.CostEstimate(
            flops=fields * 128 * 512 * (512 + 256) * 6, bytes_accessed=8 * 2**20, transcendentals=0
        ),
    )(own, other, push, *weights)


def y_kernel(fields, cells_ref, inv_ref, out_ref):
    inv = parts(inv_ref[...].T)
    rows = 2 * fields
    contract = (((1,), (1,)), ((), ()))
    dot = lambda a, b: lax.dot_general(a, b, contract, preferred_element_type=jnp.float32)
    for c in range(fields):
        for pair in range(2):
            both = []
            for z in (2 * pair, 2 * pair + 1):
                tiles = [cells_ref[pl.ds(c * 512 + 4 * tile + z, 64, stride=8), :] for tile in range(2)]
                both.append(jnp.concatenate(tiles, axis=1))
            high, low = parts(jnp.concatenate(both, axis=0))
            done = dot(inv[0], high) + (dot(inv[0], low) + dot(inv[1], high))
            out_ref[pl.ds(2 * c + pair, 256, stride=rows), :] = done


def y_solved(cells, inv_y):
    fields, x_rows, z_rows, y_cells = cells.shape
    tiles = cells.reshape(fields, x_rows, z_rows, y_cells // 128, 128).transpose(0, 1, 3, 2, 4).reshape(-1, 128)
    return pl.pallas_call(
        functools.partial(y_kernel, fields),
        out_shape=jax.ShapeDtypeStruct(tiles.shape, jnp.float32),
        in_specs=[vmem] * 2,
        out_specs=vmem,
        compiler_params=params,
        cost_estimate=pl.CostEstimate(flops=6 * tiles.size * y_cells, bytes_accessed=3 * 2**20, transcendentals=0),
    )(tiles, inv_y)


def weights_kernel(wz_ref, ix_ref, wz_high, wz_low, ix_high, ix_low):
    wz_high[...], wz_low[...] = parts(wz_ref[...])
    for yy in range(4):
        for zh in range(2):
            j = zh * 4 + yy
            rows = jnp.concatenate([ix_ref[j % 2, q, pl.ds(64 * (j // 2), 64), :] for q in range(4)], axis=1)
            at = pl.ds(64 * (2 * yy + zh), 64)
            ix_high[at, :], ix_low[at, :] = parts(rows)


def prepared(wz, ix):
    half = lambda shape: jax.ShapeDtypeStruct(shape, jnp.bfloat16)
    count = ix.shape[0] * ix.shape[2]
    return pl.pallas_call(
        weights_kernel,
        out_shape=(half(wz.shape), half(wz.shape), half((count, count)), half((count, count))),
        in_specs=[vmem] * 2,
        out_specs=(vmem,) * 4,
        compiler_params=params,
        cost_estimate=pl.CostEstimate(flops=2**20, bytes_accessed=2 * 2**20, transcendentals=0),
    )(wz, ix)


def masked_kernel(fields, got_ref, mask_ref, masked_ref, low_ref, high_ref, edge_ref):
    rows = got_ref.shape[0] // 256
    for c in range(fields):
        for pair in range(2):
            both = got_ref[pl.ds(2 * c + pair, 256, stride=rows), :].T
            for i in range(2):
                z = 2 * pair + i
                cells = both[64 * i : 64 * i + 64] * mask_ref[z]
                masked_ref[c, z] = cells
                if z == 0:
                    low_ref[c] = cells
                if z == 3:
                    high_ref[c] = cells
    edge_ref[...] = got_ref[pl.ds(rows - 1, 256, stride=rows), :].T[: 8 * fields]


def masked_cells(got, mask, fields):
    z_rows, x_rows, y_cells = mask.shape
    cells = lambda *shape: jax.ShapeDtypeStruct(shape, jnp.float32)
    return pl.pallas_call(
        functools.partial(masked_kernel, fields),
        out_shape=(
            cells(fields, z_rows, x_rows, y_cells),
            cells(fields, x_rows, y_cells),
            cells(fields, x_rows, y_cells),
            cells(2 * fields * z_rows, y_cells),
        ),
        in_specs=[vmem] * 2,
        out_specs=(vmem,) * 4,
        compiler_params=params,
        cost_estimate=pl.CostEstimate(flops=2**20, bytes_accessed=3 * 2**20, transcendentals=0),
    )(got, mask)


def stencil_kernel(fields, masked_ref, edge_ref, rim_ref, flow_ref, thick_ref, out_ref):
    row = lax.broadcasted_iota(jnp.int32, (64, 256), 0)
    lane = lax.broadcasted_iota(jnp.int32, (64, 256), 1)
    for z in range(4):
        flow_x, flow_z, flow_y = (flow_ref[i, z] for i in range(3))
        thick = thick_ref[z]
        for c in range(fields):
            k = 2 * (c * 4 + z)
            v = masked_ref[c, z]
            first = edge_ref[k : k + 1, :] * rim_ref[z : z + 1, :]
            last = edge_ref[k + 1 : k + 2, :] * rim_ref[4 + z : 5 + z, :]
            x_less = jnp.where(row == 0, first, pltpu.roll(v, 1, 0))
            x_more = jnp.where(row == 63, last, pltpu.roll(v, 63, 0))
            y_less = jnp.where(lane == 0, 0.0, pltpu.roll(v, 1, 1))
            y_more = jnp.where(lane == 255, 0.0, pltpu.roll(v, 255, 1))
            around = x_more + x_less + y_more + y_less - 6.0 * v
            slopes = flow_x * (x_more - x_less) + flow_y * (y_more - y_less)
            if z > 0:
                around, slopes = around + masked_ref[c, z - 1], slopes - flow_z * masked_ref[c, z - 1]
            if z < 3:
                around, slopes = around + masked_ref[c, z + 1], slopes + flow_z * masked_ref[c, z + 1]
            done = v + time_step * (0.5 * slopes + thick * around)
            for half in range(2):
                out_ref[pl.ds(c * 512 + half * 4 + z, 64, stride=8), :] = done[:, half * 128 : half * 128 + 128]


def rim_kernel(fields, most_ref, below_ref, above_ref, flow_ref, thick_ref, out_ref):
    low = time_step * (thick_ref[0] - 0.5 * flow_ref[1, 0])
    high = time_step * (thick_ref[3] + 0.5 * flow_ref[1, 3])
    for c in range(fields):
        for z in range(4):
            added = low * below_ref[c] if z == 0 else high * above_ref[c] if z == 3 else None
            for half in range(2):
                at = pl.ds(c * 512 + half * 4 + z, 64, stride=8)
                value = most_ref[at, :]
                out_ref[at, :] = value if added is None else value + added[:, half * 128 : half * 128 + 128]


def stencil(masked, edges, rim, below, above, flow, thick):
    fields, z_rows, x_rows, y_cells = masked.shape
    shape = jax.ShapeDtypeStruct((masked.size // 128, 128), jnp.float32)
    most = pl.pallas_call(
        functools.partial(stencil_kernel, fields),
        out_shape=shape,
        in_specs=[vmem] * 5,
        out_specs=vmem,
        compiler_params=params,
        cost_estimate=pl.CostEstimate(flops=2**23, bytes_accessed=5 * 2**20, transcendentals=0),
    )(masked, edges, rim, flow, thick)
    out = pl.pallas_call(
        functools.partial(rim_kernel, fields),
        out_shape=shape,
        in_specs=[vmem] * 5,
        out_specs=vmem,
        compiler_params=params,
        cost_estimate=pl.CostEstimate(flops=2**20, bytes_accessed=3 * 2**20, transcendentals=0),
    )(most, below, above, flow, thick)
    out = out.reshape(fields, x_rows, y_cells // 128, z_rows, 128)
    return out.transpose(0, 1, 3, 2, 4).reshape(fields, x_rows, z_rows, y_cells)


def before_and_after(head, tail, axes):
    count = lax.axis_size(axes)
    before = lax.ppermute(tail, axes, [(i, i + 1) for i in range(count - 1)])
    after = lax.ppermute(head, axes, [(i + 1, i) for i in range(count - 1)])
    return before, after


def transposed(sent):
    return lax.all_to_all(sent, chips, split_axis=0, concat_axis=0, tiled=True)


def body(
    adj_out,
    advect,
    viscosity,
    body_mask,
    marker_x,
    marker_z,
    marker_y,
    drag_weight,
    inv_x,
    inv_y,
    inv_z,
):
    fields, x_rows, z_rows, y_cells = adj_out.shape
    pair = inv_x_pair(inv_x)
    wz = z_weights(inv_z, z_rows)
    sent = y_solved(adj_out, inv_y).reshape(y_cells, -1)
    got = transposed(sent).reshape(-1, 128)
    push = push_plane(marker_x, marker_z, marker_y, drag_weight, inv_y, x_rows, z_rows)
    full_x = whole_inv_x(pair)
    weights = prepared(wz, full_x)
    mask = body_mask.astype(jnp.float32).transpose(1, 0, 2)
    rim = jnp.concatenate(before_and_after(mask[:, 0], mask[:, -1], grp), axis=0)
    flow = advect.astype(jnp.float32).transpose(0, 2, 1, 3)
    thick = viscosity.astype(jnp.float32).transpose(1, 0, 2)
    other = lax.ppermute(got, "co", swap)
    back = solve_lines(got, other, push, weights, fields)
    solved = transposed(back.reshape(y_cells, -1)).reshape(-1, 128)
    masked, low, high, edges = masked_cells(solved, mask, fields)
    below, above = before_and_after(low, high, slab)
    return stencil(masked, edges, rim, below, above, flow, thick)


def solution(mesh):
    fine = Mesh(mesh.devices.reshape(8, 4, 2, 2, 4), ("zl", "xx", "co", "zh", "yy"))
    field = P(None, grp, slab, None)
    in_specs = (field, field, P(grp, slab, None), P(grp, slab, None), P(), P(), P(), P(), P(None, grp), P(), P())

    return jax.shard_map(body, mesh=fine, in_specs=in_specs, out_specs=field, check_vma=False)
```

```python
import functools

import jax
import jax.numpy as jnp
from jax import lax
from jax.experimental import pallas as pl
from jax.experimental.pallas import tpu as pltpu
from jax.sharding import Mesh, PartitionSpec as P


time_step = 0.08
highest = lax.Precision.HIGHEST
chips = ("zl", "zh", "xx", "yy")
slab = ("zl", "xx", "co")
grp = ("zh", "yy")
swap = [(0, 1), (1, 0)]


def parts(value):
    high = value.astype(jnp.bfloat16)
    return high, (value - high.astype(jnp.float32)).astype(jnp.bfloat16)


def product(left, right):
    dot = functools.partial(jnp.dot, preferred_element_type=jnp.float32)
    return dot(left[0], right[0]) + (dot(left[0], right[1]) + dot(left[1], right[0]))


def gather_ring(block, axis):
    count = lax.axis_size(axis)
    me = lax.axis_index(axis)
    out = jnp.zeros((count,) + block.shape, block.dtype)
    out = lax.dynamic_update_index_in_dim(out, block, me, 0)
    for hop in range(1, count):
        from_it = lax.ppermute(block, axis, [(i, (i + hop) % count) for i in range(count)])
        out = lax.dynamic_update_index_in_dim(out, from_it, (me - hop) % count, 0)
    return out


def inv_x_pair(inv_x):
    pieces = lax.axis_size("xx") * lax.axis_size("co")
    depth = inv_x.shape[0] // pieces
    mine = lax.dynamic_slice_in_dim(inv_x, lax.axis_index(("xx", "co")) * depth, depth, axis=0)
    theirs = lax.ppermute(mine, "zh", swap)
    low = lax.axis_index("zh") == 0
    return jnp.concatenate([jnp.where(low, mine, theirs), jnp.where(low, theirs, mine)], axis=1)


def whole_inv_x(pair):
    for axis in ("xx", "yy", "co"):
        pair = gather_ring(pair, axis)
    return pair.reshape(*pair.shape[:2], -1, pair.shape[-1])


def z_of(k, which, half, z_rows):
    groups = half // z_rows
    depth = lax.axis_size("zl")
    group = (k % groups) % depth * (groups // depth) + (k % groups) // depth
    return group * (2 * z_rows) + which * z_rows + k // groups


def push_plane(marker_x, marker_z, marker_y, drag_weight, inv_y, x_rows, z_rows):
    y_cells = inv_y.shape[0]
    core = lax.axis_index("co")
    y_mine = lax.axis_index(chips)
    to_y = lax.dynamic_slice_in_dim(inv_y, y_mine, 1, axis=1)
    at_y = marker_y[:, None] == lax.broadcasted_iota(jnp.int32, (1, y_cells), 1)
    amount = drag_weight * jnp.dot(at_y.astype(jnp.float32), to_y, precision=highest)[:, 0]
    z_count = 2 * lax.axis_size("zl") * lax.axis_size("xx") * z_rows
    row = lax.broadcasted_iota(jnp.int32, (z_count, 1), 0)
    half = z_count // 2
    z_row = jnp.where(row < half, z_of(row, core, half, z_rows), z_of(row - half, 1 - core, half, z_rows))
    y_size, h_size = lax.axis_size("yy"), lax.axis_size("zh")
    lane = lax.broadcasted_iota(jnp.int32, (1, y_size * h_size * x_rows), 1)
    block = lane // x_rows
    x_lane = ((block % h_size) * y_size + block // h_size) * x_rows + lane % x_rows
    at_z = (z_row == marker_z[None, :]).astype(jnp.float32)
    at_x = jnp.where(marker_x[:, None] == x_lane, amount[:, None], 0.0)
    return jnp.dot(at_z, at_x, precision=highest)


def z_weights(inv_z, z_rows):
    count = inv_z.shape[0]
    half = count // 2
    core = lax.axis_index("co")

    def chosen(which):
        k = lax.broadcasted_iota(jnp.int32, (half, count), 0)
        z = lax.broadcasted_iota(jnp.int32, (half, count), 1)
        return (z == z_of(k, which, half, z_rows)).astype(jnp.float32)

    mine = chosen(core)
    both = jnp.concatenate([mine, chosen(1 - core)], axis=0)
    picked = jnp.einsum("az,zw->aw", both, inv_z, precision=highest)
    return jnp.einsum("bw,aw->ba", mine, picked, precision=highest)


def solve_kernel(fields, own_ref, other_ref, push_ref, wz_high, wz_low, ix_high, ix_low, out_ref, z_ref, edge_ref):
    rows = own_ref.shape[0] // 256
    out_rows = out_ref.shape[0] // 256
    lane = lax.broadcasted_iota(jnp.int32, (32, 128), 1)
    low_half = lane < 64

    def messages(zh, yy, depth, row):
        return [pl.ds((zh * 16 + xx * 4 + yy) * depth + row, 8, stride=32 * depth) for xx in range(4)]

    def put(zh, yy, row, value):
        for i, at in enumerate(messages(zh, yy, out_rows, row)):
            out_ref[at, :] = value[8 * i : 8 * i + 8]

    def lines(ref, c):
        evens, odds = [None, None], [None, None]
        for pair in range(2):
            even, odd = [], []
            for q in range(4):
                first = jnp.concatenate([ref[at, :] for at in messages(0, q, rows, 2 * c + pair)], axis=0)
                second = jnp.concatenate([ref[at, :] for at in messages(1, q, rows, 2 * c + pair)], axis=0)
                even.append(jnp.where(low_half, first, pltpu.roll(second, 64, 1)))
                odd.append(jnp.where(low_half, pltpu.roll(first, 64, 1), second))
            evens[pair] = jnp.concatenate(even, axis=1)
            odds[pair] = jnp.concatenate(odd, axis=1)
        return jnp.concatenate([evens[0], odds[0], evens[1], odds[1]], axis=0)

    wz = wz_high[...], wz_low[...]
    for c in range(fields):
        both = jnp.concatenate([lines(own_ref, c), lines(other_ref, c)], axis=0)
        if c == 0:
            both = both + push_ref[...]
        z_ref[pl.ds(c * 128, 128), :] = product(wz, parts(both))
    ix = ix_high[...], ix_low[...]
    edge_ref[...] = jnp.zeros_like(edge_ref)
    for c in range(fields):
        done = product(parts(z_ref[pl.ds(c * 128, 128), :]), ix)
        for pair in range(2):
            for q in range(4):
                two = [done[(2 * pair + i) * 32 : (2 * pair + i + 1) * 32, q * 128 : q * 128 + 128] for i in range(2)]
                first = jnp.where(low_half, two[0], pltpu.roll(two[1], 64, 1))
                second = jnp.where(low_half, pltpu.roll(two[0], 64, 1), two[1])
                put(0, q, 2 * c + pair, first)
                put(1, q, 2 * c + pair, second)
                for i in range(2):
                    k = c * 4 + 2 * pair + i
                    outer = pltpu.roll(two[i], 2 * k + 1, 1)
                    inner = pltpu.roll(two[i], (2 * k + 65) % 128, 1)
                    for target, value, spot in (
                        (q - 1, outer, 2 * k + 1),
                        (q + 4 + 1, outer, 2 * k),
                        (q + 4 - 1, inner, 2 * k + 1),
                        (q + 1, inner, 2 * k),
                    ):
                        if 0 <= target < 8:
                            edge_ref[target] = jnp.where(lane == spot, value, edge_ref[target])
    for g in range(8):
        put(g // 4, g % 4, out_rows - 1, edge_ref[g])


vmem = pl.BlockSpec(memory_space=pltpu.VMEM)
params = pltpu.CompilerParams(vmem_limit_bytes=24 * 2**20)


def solve_lines(own, other, push, weights, fields):
    return pl.pallas_call(
        functools.partial(solve_kernel, fields),
        out_shape=jax.ShapeDtypeStruct((own.shape[0] + 256, 128), jnp.float32),
        in_specs=[vmem] * 7,
        out_specs=vmem,
        scratch_shapes=[pltpu.VMEM((fields * 128, 512), jnp.float32), pltpu.VMEM((8, 32, 128), jnp.float32)],
        compiler_params=params,
        cost_estimate=pl.CostEstimate(
            flops=fields * 128 * 512 * (512 + 256) * 6, bytes_accessed=8 * 2**20, transcendentals=0
        ),
    )(own, other, push, *weights)


def y_kernel(fields, cells_ref, inv_ref, out_ref):
    inv = parts(inv_ref[...].T)
    rows = 2 * fields
    contract = (((1,), (1,)), ((), ()))
    dot = lambda a, b: lax.dot_general(a, b, contract, preferred_element_type=jnp.float32)
    for c in range(fields):
        for pair in range(2):
            both = []
            for z in (2 * pair, 2 * pair + 1):
                tiles = [cells_ref[pl.ds(c * 512 + 4 * tile + z, 64, stride=8), :] for tile in range(2)]
                both.append(jnp.concatenate(tiles, axis=1))
            high, low = parts(jnp.concatenate(both, axis=0))
            done = dot(inv[0], high) + (dot(inv[0], low) + dot(inv[1], high))
            out_ref[pl.ds(2 * c + pair, 256, stride=rows), :] = done


def y_solved(cells, inv_y):
    fields, x_rows, z_rows, y_cells = cells.shape
    tiles = cells.reshape(fields, x_rows, z_rows, y_cells // 128, 128).transpose(0, 1, 3, 2, 4).reshape(-1, 128)
    return pl.pallas_call(
        functools.partial(y_kernel, fields),
        out_shape=jax.ShapeDtypeStruct(tiles.shape, jnp.float32),
        in_specs=[vmem] * 2,
        out_specs=vmem,
        compiler_params=params,
        cost_estimate=pl.CostEstimate(flops=6 * tiles.size * y_cells, bytes_accessed=3 * 2**20, transcendentals=0),
    )(tiles, inv_y)


def weights_kernel(wz_ref, ix_ref, wz_high, wz_low, ix_high, ix_low):
    wz_high[...], wz_low[...] = parts(wz_ref[...])
    for yy in range(4):
        for zh in range(2):
            j = zh * 4 + yy
            rows = jnp.concatenate([ix_ref[j % 2, q, pl.ds(64 * (j // 2), 64), :] for q in range(4)], axis=1)
            at = pl.ds(64 * (2 * yy + zh), 64)
            ix_high[at, :], ix_low[at, :] = parts(rows)


def prepared(wz, ix):
    half = lambda shape: jax.ShapeDtypeStruct(shape, jnp.bfloat16)
    count = ix.shape[0] * ix.shape[2]
    return pl.pallas_call(
        weights_kernel,
        out_shape=(half(wz.shape), half(wz.shape), half((count, count)), half((count, count))),
        in_specs=[vmem] * 2,
        out_specs=(vmem,) * 4,
        compiler_params=params,
        cost_estimate=pl.CostEstimate(flops=2**20, bytes_accessed=2 * 2**20, transcendentals=0),
    )(wz, ix)


def masked_kernel(fields, got_ref, mask_ref, masked_ref, low_ref, high_ref, edge_ref):
    rows = got_ref.shape[0] // 256
    for c in range(fields):
        for pair in range(2):
            both = got_ref[pl.ds(2 * c + pair, 256, stride=rows), :].T
            for i in range(2):
                z = 2 * pair + i
                cells = both[64 * i : 64 * i + 64] * mask_ref[z]
                masked_ref[c, z] = cells
                if z == 0:
                    low_ref[c] = cells
                if z == 3:
                    high_ref[c] = cells
    edge_ref[...] = got_ref[pl.ds(rows - 1, 256, stride=rows), :].T[: 8 * fields]


def masked_cells(got, mask, fields):
    z_rows, x_rows, y_cells = mask.shape
    cells = lambda *shape: jax.ShapeDtypeStruct(shape, jnp.float32)
    return pl.pallas_call(
        functools.partial(masked_kernel, fields),
        out_shape=(
            cells(fields, z_rows, x_rows, y_cells),
            cells(fields, x_rows, y_cells),
            cells(fields, x_rows, y_cells),
            cells(2 * fields * z_rows, y_cells),
        ),
        in_specs=[vmem] * 2,
        out_specs=(vmem,) * 4,
        compiler_params=params,
        cost_estimate=pl.CostEstimate(flops=2**20, bytes_accessed=3 * 2**20, transcendentals=0),
    )(got, mask)


def stencil_kernel(fields, masked_ref, edge_ref, rim_ref, flow_ref, thick_ref, out_ref):
    row = lax.broadcasted_iota(jnp.int32, (64, 256), 0)
    lane = lax.broadcasted_iota(jnp.int32, (64, 256), 1)
    for z in range(4):
        flow_x, flow_z, flow_y = (flow_ref[i, z] for i in range(3))
        thick = thick_ref[z]
        for c in range(fields):
            k = 2 * (c * 4 + z)
            v = masked_ref[c, z]
            first = edge_ref[k : k + 1, :] * rim_ref[z : z + 1, :]
            last = edge_ref[k + 1 : k + 2, :] * rim_ref[4 + z : 5 + z, :]
            x_less = jnp.where(row == 0, first, pltpu.roll(v, 1, 0))
            x_more = jnp.where(row == 63, last, pltpu.roll(v, 63, 0))
            y_less = jnp.where(lane == 0, 0.0, pltpu.roll(v, 1, 1))
            y_more = jnp.where(lane == 255, 0.0, pltpu.roll(v, 255, 1))
            around = x_more + x_less + y_more + y_less - 6.0 * v
            slopes = flow_x * (x_more - x_less) + flow_y * (y_more - y_less)
            if z > 0:
                around, slopes = around + masked_ref[c, z - 1], slopes - flow_z * masked_ref[c, z - 1]
            if z < 3:
                around, slopes = around + masked_ref[c, z + 1], slopes + flow_z * masked_ref[c, z + 1]
            done = v + time_step * (0.5 * slopes + thick * around)
            for half in range(2):
                out_ref[pl.ds(c * 512 + half * 4 + z, 64, stride=8), :] = done[:, half * 128 : half * 128 + 128]


def rim_kernel(fields, most_ref, below_ref, above_ref, flow_ref, thick_ref, out_ref):
    low = time_step * (thick_ref[0] - 0.5 * flow_ref[1, 0])
    high = time_step * (thick_ref[3] + 0.5 * flow_ref[1, 3])
    for c in range(fields):
        for z in range(4):
            added = low * below_ref[c] if z == 0 else high * above_ref[c] if z == 3 else None
            for half in range(2):
                at = pl.ds(c * 512 + half * 4 + z, 64, stride=8)
                value = most_ref[at, :]
                out_ref[at, :] = value if added is None else value + added[:, half * 128 : half * 128 + 128]


def stencil(masked, edges, rim, below, above, flow, thick):
    fields, z_rows, x_rows, y_cells = masked.shape
    shape = jax.ShapeDtypeStruct((masked.size // 128, 128), jnp.float32)
    most = pl.pallas_call(
        functools.partial(stencil_kernel, fields),
        out_shape=shape,
        in_specs=[vmem] * 5,
        out_specs=vmem,
        compiler_params=params,
        cost_estimate=pl.CostEstimate(flops=2**23, bytes_accessed=5 * 2**20, transcendentals=0),
    )(masked, edges, rim, flow, thick)
    out = pl.pallas_call(
        functools.partial(rim_kernel, fields),
        out_shape=shape,
        in_specs=[vmem] * 5,
        out_specs=vmem,
        compiler_params=params,
        cost_estimate=pl.CostEstimate(flops=2**20, bytes_accessed=3 * 2**20, transcendentals=0),
    )(most, below, above, flow, thick)
    out = out.reshape(fields, x_rows, y_cells // 128, z_rows, 128)
    return out.transpose(0, 1, 3, 2, 4).reshape(fields, x_rows, z_rows, y_cells)


def before_and_after(head, tail, axes):
    count = lax.axis_size(axes)
    before = lax.ppermute(tail, axes, [(i, i + 1) for i in range(count - 1)])
    after = lax.ppermute(head, axes, [(i + 1, i) for i in range(count - 1)])
    return before, after


def transposed(sent):
    return lax.all_to_all(sent, chips, split_axis=0, concat_axis=0, tiled=True)


def body(
    adj_out,
    advect,
    viscosity,
    body_mask,
    marker_x,
    marker_z,
    marker_y,
    drag_weight,
    inv_x,
    inv_y,
    inv_z,
):
    fields, x_rows, z_rows, y_cells = adj_out.shape
    pair = inv_x_pair(inv_x)
    wz = z_weights(inv_z, z_rows)
    sent = y_solved(adj_out, inv_y).reshape(y_cells, -1)
    got = transposed(sent).reshape(-1, 128)
    push = push_plane(marker_x, marker_z, marker_y, drag_weight, inv_y, x_rows, z_rows)
    full_x = whole_inv_x(pair)
    weights = prepared(wz, full_x)
    mask = body_mask.astype(jnp.float32).transpose(1, 0, 2)
    rim = jnp.concatenate(before_and_after(mask[:, 0], mask[:, -1], grp), axis=0)
    flow = advect.astype(jnp.float32).transpose(0, 2, 1, 3)
    thick = viscosity.astype(jnp.float32).transpose(1, 0, 2)
    other = lax.ppermute(got, "co", swap)
    back = solve_lines(got, other, push, weights, fields)
    solved = transposed(back.reshape(y_cells, -1)).reshape(-1, 128)
    masked, low, high, edges = masked_cells(solved, mask, fields)
    below, above = before_and_after(low, high, slab)
    return stencil(masked, edges, rim, below, above, flow, thick)


def solution(mesh):
    fine = Mesh(mesh.devices.reshape(8, 4, 2, 2, 4), ("zl", "xx", "co", "zh", "yy"))
    field = P(None, grp, slab, None)
    in_specs = (field, field, P(grp, slab, None), P(grp, slab, None), P(), P(), P(), P(), P(None, grp), P(), P())

    return jax.shard_map(body, mesh=fine, in_specs=in_specs, out_specs=field, check_vma=False)
```
